32 devices in a mesh: row: 4 (over x, core), col: 8 (over z, y).
Axes of the slice: x: 2, y: 2, z: 4, core: 2. Of those that a mesh axis runs over, the one named last changes fastest.
Arguments:
- tile_weight: bfloat16 [32, 32, 2, 128, 128], P(('row', 'col')), may hold values from 0.049804688 to 1
- tile_angle: bfloat16 [32, 32, 2, 128, 128], P(('row', 'col')), may hold values from -3.140625 to 3.140625
- tile_list: int32 [32, 32, 2, 2], P(('row', 'col')), may hold values from 0 to 63, as said below
- tile_count: int32 [32, 32], P(('row', 'col')), may hold values from 0 to 2, as said below
- init_basis: float32 [2, 32, 8192], P(None, None, ('row', 'col')), may hold values from -6 to 6
Outputs:
- basis: float32 [2, 32, 8192], P(None, None, ('row', 'col'))
The draws below stay inside these ranges and needn't reach their ends.
Inputs may be any that keep to these rules, and one draw needn't show every extreme that they name: `tile_list`: let piece(b) = b // 2 for a block b, and number devices s = a * 8 + e' along row+col. For device s = a * 8 + b' and destination d = f * 8 + e, slot [s, d, k] holds I with piece(I) = a * 8 + e and J with piece(J) = f * 8 + b'. The slots of one s, d hold distinct tiles; for d = s they hold the diagonal tiles (I, I) of the first 2 blocks of the device's piece. tile_count[s, s] = 2, and one destination has 2 live slots from every device.
All inputs are finite; a program needn't handle non-finite values.
Results may differ from the reference program's by a relative error of at most 0.0053.
Values may be sent and summed in bfloat16 or wider, within the bound.
A program may use at most 256 MiB of HBM per device.

```python
import math
import jax
import jax.numpy as jnp
from jax import lax

TILE = 128
BASIS = 32
BLK_DEV = 2
PAIR_CAP = 2
ITERS = 3
GRID_COLS = 8
IMAGES = 8192
DEVICES = 32


def draw_tile_list(key, part):
    source = jnp.arange(DEVICES)[:, None]
    target = jnp.arange(DEVICES)[None, :]
    src_row = source // GRID_COLS
    src_col = source % GRID_COLS
    dst_row = target // GRID_COLS
    dst_col = target % GRID_COLS
    piece_rows = src_row * GRID_COLS + dst_col
    segment_columns = dst_row * GRID_COLS + src_col
    combos = BLK_DEV * BLK_DEV
    scores = jax.random.randint(jax.random.fold_in(key, 11), (DEVICES, DEVICES, combos), 0, 1 << 20) * combos + jnp.arange(combos)[None, None, :]
    order = jnp.argsort(scores, axis=-1)[:, :, :PAIR_CAP]
    offset_row = order // BLK_DEV
    offset_col = order % BLK_DEV
    same = (source == target)[:, :, None]
    slots = jnp.arange(PAIR_CAP)[None, None, :]
    offset_row = jnp.where(same, slots, offset_row)
    offset_col = jnp.where(same, slots, offset_col)
    rows = piece_rows[:, :, None] * BLK_DEV + offset_row
    cols = segment_columns[:, :, None] * BLK_DEV + offset_col
    return jnp.stack([rows, cols], -1).astype(jnp.int32)


def draw_tile_count(key, part):
    counts = jax.random.randint(jax.random.fold_in(key, 21), (DEVICES, DEVICES), 0, PAIR_CAP + 1)
    busiest = jax.random.randint(jax.random.fold_in(key, 22), (), 0, DEVICES)
    places = jnp.arange(DEVICES)
    full = (places[None, :] == busiest) | (places[:, None] == places[None, :])
    return jnp.where(full, PAIR_CAP, counts).astype(jnp.int32)


def shard_levels(key, extent, split, smallest, top_value):
    def one(axis_at, shards_of):
        heights = jax.random.uniform(jax.random.fold_in(jax.random.fold_in(key, 6), axis_at), (shards_of,), jnp.float32, smallest / len(split), top_value / len(split))
        return jnp.repeat(jnp.exp(heights), extent[axis_at] // shards_of).reshape((-1,) + (1,) * (len(extent) - axis_at - 1))

    gain = one(*split[0])
    for cut in split[1:]:
        gain = gain * one(*cut)
    return gain


def gaussian(key, extent, spread, most, shards=(), held_as=jnp.bfloat16):
    values = spread * jax.random.normal(key, extent, jnp.float32)
    if shards:
        values = values * shard_levels(key, extent, shards, -0.22, 0.18)
    return jnp.clip(values, -most, most).astype(held_as)


def setup_inputs(seed: int = 0) -> dict:
    arg_keys = jax.random.split(jax.random.key(seed), 6)
    return {
        "tile_weight": jnp.clip(jnp.exp(math.log(1.0) - 2.9996462 * jax.random.uniform(arg_keys[0], (DEVICES, DEVICES, PAIR_CAP, TILE, TILE), jnp.float32) ** shard_levels(arg_keys[0], (DEVICES, DEVICES, PAIR_CAP, TILE, TILE), ((0, 32),), -0.2, 0.2)), 0.049804688, 1.0).astype(jnp.bfloat16),
        "tile_angle": jnp.clip(jax.random.uniform(arg_keys[1], (DEVICES, DEVICES, PAIR_CAP, TILE, TILE), jnp.float32, -3.140625, 3.140625), -3.140625, 3.140625).astype(jnp.bfloat16),
        "tile_list": draw_tile_list(jax.random.fold_in(arg_keys[5], 71), 0),
        "tile_count": draw_tile_count(jax.random.fold_in(arg_keys[5], 71), 0),
        "init_basis": gaussian(arg_keys[4], (2, BASIS, IMAGES), 1.0, 6.0, ((2, 32),), jnp.float32),
    }


def complex_tiles(weight, angle):
    weight_f = weight.astype(jnp.float32)
    angle_f = angle.astype(jnp.float32)
    return ((weight_f * jnp.cos(angle_f)).astype(jnp.bfloat16), (weight_f * jnp.sin(angle_f)).astype(jnp.bfloat16))

def highest_dot(left, right):
    return jnp.dot(left, right, precision=lax.Precision.HIGHEST, preferred_element_type=jnp.float32)

def gram_terms(image_real, image_imag):
    gram_real = highest_dot(image_real, image_real.T) + highest_dot(image_imag, image_imag.T)
    gram_imag = highest_dot(image_real, image_imag.T) - highest_dot(image_imag, image_real.T)
    return (gram_real, gram_imag)

def orthonormal(gram_real, gram_imag, image_real, image_imag):
    width = gram_real.shape[0]
    indices = jnp.arange(width)
    ridge = 0.01 * jnp.trace(gram_real) / width + 1e-06
    gram_real = gram_real + ridge * jnp.eye(width, dtype=jnp.float32)
    lower_real = jnp.zeros((width, width), jnp.float32)
    lower_imag = jnp.zeros((width, width), jnp.float32)
    for column in range(width):
        prod_real = highest_dot(lower_real, lower_real[column]) + highest_dot(lower_imag, lower_imag[column])
        prod_imag = highest_dot(lower_imag, lower_real[column]) - highest_dot(lower_real, lower_imag[column])
        pivot = jnp.sqrt(gram_real[column, column] - prod_real[column])
        below = indices > column
        col_real = (gram_real[:, column] - prod_real) / pivot
        col_imag = (gram_imag[:, column] - prod_imag) / pivot
        lower_real = lower_real.at[:, column].set(jnp.where(below, col_real, jnp.where(indices == column, pivot, 0.0)))
        lower_imag = lower_imag.at[:, column].set(jnp.where(below, col_imag, 0.0))
    inv_real = jnp.zeros((width, width), jnp.float32)
    inv_imag = jnp.zeros((width, width), jnp.float32)
    for column in range(width):
        unit = (indices == column).astype(jnp.float32)
        sum_real = highest_dot(lower_real[column], inv_real) - highest_dot(lower_imag[column], inv_imag)
        sum_imag = highest_dot(lower_real[column], inv_imag) + highest_dot(lower_imag[column], inv_real)
        diag_value = lower_real[column, column]
        inv_real = inv_real.at[column].set((unit - sum_real) / diag_value)
        inv_imag = inv_imag.at[column].set(-sum_imag / diag_value)
    new_real = highest_dot(inv_real, image_real) + highest_dot(inv_imag, image_imag)
    new_imag = highest_dot(inv_real, image_imag) - highest_dot(inv_imag, image_real)
    return jnp.stack([new_real, new_imag], 0)

def reference(tile_weight, tile_angle, tile_list, tile_count, init_basis):
    blocks_all = IMAGES // TILE
    slot_count = DEVICES * PAIR_CAP
    listing = tile_list.reshape(DEVICES, slot_count, 2).astype(jnp.int32)
    alive = (jnp.arange(PAIR_CAP)[None, None, :] < tile_count[:, :, None]).reshape(DEVICES, slot_count)
    halves = jnp.where(alive, 0.5, 0.0).astype(jnp.float32)
    weights = tile_weight.reshape(DEVICES, slot_count, TILE, TILE)
    angles = tile_angle.reshape(DEVICES, slot_count, TILE, TILE)

    def degree_step(carry, item):
        weight, pairs, half_w = item
        row_sums = lax.optimization_barrier(jnp.sum(weight.astype(jnp.float32), axis=2))
        col_sums = lax.optimization_barrier(jnp.sum(weight.astype(jnp.float32), axis=1))
        carry = carry.at[pairs[:, 0]].add(half_w[:, None] * row_sums)
        carry = carry.at[pairs[:, 1]].add(half_w[:, None] * col_sums)
        return (carry, None)
    degree, _ = lax.scan(degree_step, jnp.zeros((blocks_all, TILE), jnp.float32), (weights, listing, halves))
    scale = lax.rsqrt(degree)
    basis = init_basis.astype(jnp.float32)
    for rounds in range(ITERS):
        scaled = (basis.reshape(2, BASIS, blocks_all, TILE) * scale[None, None]).astype(jnp.bfloat16)
        blocks = jnp.transpose(scaled, (2, 0, 1, 3))

        def apply_step(carry, item):
            weight, angle, pairs, half_w = item
            real_part, imag_part = complex_tiles(weight, angle)
            real_factor = real_part.astype(jnp.float32)
            imaginary_factor = imag_part.astype(jnp.float32)
            from_cols = blocks[pairs[:, 1]].astype(jnp.float32)
            source_row_blocks = blocks[pairs[:, 0]].astype(jnp.float32)
            fwd_a = jnp.einsum('nskj,nij->nski', from_cols, real_factor)
            fwd_b = jnp.einsum('nskj,nij->nski', from_cols, imaginary_factor)
            forward = jnp.stack([fwd_a[:, 0] - fwd_b[:, 1], fwd_a[:, 1] + fwd_b[:, 0]], 1)
            reflected_first = jnp.einsum('chqr,crg->chqg', source_row_blocks, real_factor)
            reflected_second = jnp.einsum('chqr,crg->chqg', source_row_blocks, imaginary_factor)
            reflected_tile = jnp.stack([reflected_first[:, 0] + reflected_second[:, 1], reflected_first[:, 1] - reflected_second[:, 0]], 1)
            carry = carry.at[pairs[:, 0]].add(half_w[:, None, None, None] * forward)
            carry = carry.at[pairs[:, 1]].add(half_w[:, None, None, None] * reflected_tile)
            return (carry, None)
        image, _ = lax.scan(apply_step, jnp.zeros((blocks_all, 2, BASIS, TILE), jnp.float32), (weights, angles, listing, halves))
        image = image * scale[:, None, None, :]
        image = jnp.transpose(image, (1, 2, 0, 3)).reshape(2, BASIS, IMAGES)
        gram_real, gram_imag = gram_terms(image[0], image[1])
        basis = orthonormal(gram_real / IMAGES, gram_imag / IMAGES, image[0], image[1])
    return basis
```

```python
import functools
import jax
import jax.numpy as jnp
from jax import lax
from jax.experimental import pallas as pl
from jax.experimental.pallas import tpu as pltpu
from jax.sharding import PartitionSpec as P

ITERS = 3
PART_DTYPE = jnp.bfloat16
MESH = pl.DeviceIdType.MESH
HIGH = lax.Precision.HIGHEST
NT = (((1,), (1,)), ((), ()))
NN = (((1,), (0,)), ((), ()))

SIN_TERMS = (-1.0 / 39916800, 1.0 / 362880, -1.0 / 5040, 1.0 / 120, -1.0 / 6, 1.0)
COS_TERMS = (1.0 / 479001600, -1.0 / 3628800, 1.0 / 40320, -1.0 / 720, 1.0 / 24, -0.5, 1.0)


def horner(terms, x):
    total = jnp.full_like(x, terms[0])
    for term in terms[1:]:
        total = total * x + term
    return total


def dot(left, right, dims, precision=None):
    return lax.dot_general(left, right, dims, precision=precision, preferred_element_type=jnp.float32)


def prep_kernel(cols, cap, per, tile, list_ref, count_ref, weight_ref, angle_ref, real_ref, imag_ref, rdeg_ref, cdeg_ref, held):
    f = pl.program_id(0)
    piece = per * tile

    @pl.when(f == 0)
    def _():
        rdeg_ref[...] = jnp.zeros_like(rdeg_ref)

    cdeg_ref[...] = jnp.zeros_like(cdeg_ref)
    real_ref[...] = jnp.zeros_like(real_ref)
    imag_ref[...] = jnp.zeros_like(imag_ref)
    ones = jnp.ones((8, piece), jnp.bfloat16)

    def step(e, carry):
        d = f * cols + e
        held[...] = jnp.zeros_like(held)
        for k in range(cap):

            @pl.when(k < count_ref[d])
            def _():
                at = (d * cap + k) * 2
                row_off = lax.rem(list_ref[at], per)
                col_off = lax.rem(list_ref[at + 1], per)
                weight = weight_ref[e, k]
                w = weight.astype(jnp.float32)
                half = angle_ref[e, k].astype(jnp.float32) * 0.5
                square = half * half
                sin_half = half * horner(SIN_TERMS, square)
                cos_half = horner(COS_TERMS, square)
                cos_full = 1.0 - 2.0 * (sin_half * sin_half)
                sin_full = 2.0 * (sin_half * cos_half)
                rows = pl.ds(pl.multiple_of(e * piece + row_off * tile, tile), tile)
                lanes = pl.ds(pl.multiple_of(col_off * tile, tile), tile)
                real_ref[rows, lanes] = (w * cos_full).astype(jnp.bfloat16)
                imag_ref[rows, lanes] = (w * sin_full).astype(jnp.bfloat16)
                held[pl.ds(pl.multiple_of(row_off * tile, tile), tile), lanes] = weight

        block = held[...]
        rdeg_ref[e] += dot(ones, block, NT)
        cdeg_ref[0] += dot(ones, block, NN)
        return carry

    lax.fori_loop(0, cols, step, 0)


def main_kernel(
    rows, cols, images_all, width, real_any, imag_any, rdeg_ref, cdeg_ref, init_ref, out_ref,
    real, imag, rdeg_recv, cdeg_recv, xsend, xrow, xcol, fsend, frecv, msend, mrecv,
    grow_send, grow, gcol_send, gcol, basis, scales,
    load_sem, drs, drr, dcs, dcr, xrs, xrr, xcs, xcr, fs, fr, ms, mr_, grs, grr, gcs, gcr,
):
    a = lax.axis_index("row")
    b = lax.axis_index("col")
    piece = init_ref.shape[1]

    def row_peer(k):
        return lax.rem(a + k, rows)

    def col_peer(k):
        return lax.rem(b + k, cols)

    def row_copy(src, dst, ssem, rsem, k):
        return pltpu.make_async_remote_copy(
            src_ref=src, dst_ref=dst.at[a], send_sem=ssem.at[k], recv_sem=rsem.at[k],
            device_id=(row_peer(k), b), device_id_type=MESH)

    def col_copy(src, dst, ssem, rsem, k):
        return pltpu.make_async_remote_copy(
            src_ref=src, dst_ref=dst.at[b], send_sem=ssem.at[k], recv_sem=rsem.at[k],
            device_id=(a, col_peer(k)), device_id_type=MESH)

    loads = [pltpu.make_async_copy(real_any, real, load_sem.at[0]),
             pltpu.make_async_copy(imag_any, imag, load_sem.at[1])]
    for load in loads:
        load.start()

    barrier = pltpu.get_barrier_semaphore()
    for k in range(1, rows):
        pl.semaphore_signal(barrier, inc=1, device_id=(row_peer(k), b), device_id_type=MESH)
    for k in range(1, cols):
        pl.semaphore_signal(barrier, inc=1, device_id=(a, col_peer(k)), device_id_type=MESH)
    pl.semaphore_wait(barrier, rows + cols - 2)

    copies = [col_copy(rdeg_ref.at[col_peer(k)], rdeg_recv, dcs, dcr, k) for k in range(1, cols)]
    copies += [row_copy(cdeg_ref.at[row_peer(k)], cdeg_recv, drs, drr, k) for k in range(1, rows)]
    for copy in copies:
        copy.start()
    rdeg_recv[b] = rdeg_ref[b]
    cdeg_recv[a] = cdeg_ref[a]
    basis[...] = init_ref[...]
    for copy in copies:
        copy.wait()
    degree = rdeg_recv[0]
    for e in range(1, cols):
        degree = degree + rdeg_recv[e]
    for f in range(rows):
        degree = degree + cdeg_recv[f]
    scales[...] = 1.0 / jnp.sqrt(0.5 * degree)
    for load in loads:
        load.wait()

    def turned(x):
        return jnp.concatenate([-x[width:], x[:width]], 0)

    row_id = lax.broadcasted_iota(jnp.int32, (width, 4 * width), 0)
    lane_id = lax.broadcasted_iota(jnp.int32, (width, 4 * width), 1)

    def iteration(t, carry):
        scale = scales[0:1]
        xs = (basis[...] * scale).astype(jnp.bfloat16)
        xsend[...] = xs
        row_x = [row_copy(xsend, xrow, xrs, xrr, k) for k in range(1, rows)]
        col_x = [col_copy(xsend, xcol, xcs, xcr, k) for k in range(1, cols)]
        for copy in row_x + col_x:
            copy.start()
        xrow[a] = xs
        xcol[b] = xs
        for copy in row_x:
            copy.wait_recv()

        def forward(e):
            total = None
            at = pl.ds(pl.multiple_of(e * piece, piece), piece)
            for f in range(rows):
                x = xrow[f]
                lanes = slice(f * piece, (f + 1) * piece)
                term = dot(x, real[at, lanes], NT) + dot(turned(x), imag[at, lanes], NT)
                total = term if total is None else total + term
            return total.astype(fsend.dtype)

        def forward_step(k, carry):
            fsend[k] = forward(col_peer(k))
            col_copy(fsend.at[k], frecv, fs, fr, k).start()
            return carry

        lax.fori_loop(1, cols, forward_step, 0)
        frecv[b] = forward(b)
        for copy in col_x:
            copy.wait_recv()

        def mirror(f):
            total = None
            lanes = pl.ds(pl.multiple_of(f * piece, piece), piece)
            for e in range(cols):
                x = xcol[e]
                at = slice(e * piece, (e + 1) * piece)
                term = dot(x, real[at, lanes], NN) - dot(turned(x), imag[at, lanes], NN)
                total = term if total is None else total + term
            return total.astype(msend.dtype)

        def mirror_step(k, carry):
            msend[k] = mirror(row_peer(k))
            row_copy(msend.at[k], mrecv, ms, mr_, k).start()
            return carry

        lax.fori_loop(1, rows, mirror_step, 0)
        mrecv[a] = mirror(a)
        for copy in row_x + col_x:
            copy.wait_send()
        for k in range(1, cols):
            col_copy(fsend.at[k], frecv, fs, fr, k).wait()
        for k in range(1, rows):
            row_copy(msend.at[k], mrecv, ms, mr_, k).wait()
        total = frecv[0].astype(jnp.float32)
        for e in range(1, cols):
            total = total + frecv[e].astype(jnp.float32)
        for f in range(rows):
            total = total + mrecv[f].astype(jnp.float32)
        image = total * (0.5 * scale)

        first, second = image[:width], image[width:]
        both = jnp.concatenate([first, second], 1)
        other = jnp.concatenate([second, -first], 1)
        right = jnp.concatenate([both, other, jnp.zeros((2 * width, 2 * piece), jnp.float32)], 0)
        gram = dot(both, right, NT, HIGH)
        upper = width // 2
        packed = gram[:upper] + pltpu.roll(gram[upper:], 2 * width, 1)
        grow_send[...] = packed
        gram_row = [row_copy(grow_send, grow, grs, grr, k) for k in range(1, rows)]
        for copy in gram_row:
            copy.start()
        grow[a] = packed
        for copy in gram_row:
            copy.wait()
        packed = grow[0]
        for f in range(1, rows):
            packed = packed + grow[f]
        gcol_send[...] = packed
        gram_col = [col_copy(gcol_send, gcol, gcs, gcr, k) for k in range(1, cols)]
        for copy in gram_col:
            copy.start()
        gcol[b] = packed
        for copy in gram_col:
            copy.wait()
        packed = gcol[0]
        for e in range(1, cols):
            packed = packed + gcol[e]
        packed = packed / images_all
        gram = jnp.concatenate([packed, pltpu.roll(packed, 2 * width, 1)], 0)
        inside = lane_id < width
        on_diag = lane_id == row_id
        trace = jnp.sum(jnp.where(on_diag, gram, 0.0), axis=(0, 1), keepdims=True)
        ridge = 0.01 * trace / width + 1e-06
        ar = jnp.where(inside, gram, jnp.where(lane_id == row_id + width, 1.0, 0.0))
        ar = ar + jnp.where(on_diag, ridge, 0.0)
        ai = jnp.where(inside, pltpu.roll(gram, 3 * width, 1), 0.0)
        for c in range(width):
            below = row_id[:, 0:1] > c
            inverse = 1.0 / ar[c:c + 1, c:c + 1]
            fac_r = jnp.where(below, ar[:, c:c + 1], 0.0)
            fac_i = jnp.where(below, ai[:, c:c + 1], 0.0)
            top_r = ar[c:c + 1] * inverse
            top_i = ai[c:c + 1] * inverse
            ar = ar - (fac_r * top_r - fac_i * top_i)
            ai = ai - (fac_r * top_i + fac_i * top_r)
        pivots = jnp.sum(jnp.where(on_diag, ar, 0.0), axis=1, keepdims=True)
        roots = 1.0 / jnp.sqrt(pivots)
        ar = ar * roots
        ai = ai * roots
        top = jnp.where(inside, pltpu.roll(ar, 3 * width, 1), ai)
        bottom = jnp.where(inside, -pltpu.roll(ai, 3 * width, 1), ar)
        left = jnp.concatenate([top, bottom], 0)[:, :2 * width]
        basis[...] = dot(left, image, NN, HIGH)
        return carry

    lax.fori_loop(0, ITERS, iteration, 0)
    out_ref[...] = basis[...]


def shards(tile_weight, tile_angle, tile_list, tile_count, init_basis):
    rows = lax.axis_size("row")
    cols = lax.axis_size("col")
    devices = rows * cols
    tile = tile_weight.shape[-1]
    cap = tile_weight.shape[2]
    width = init_basis.shape[1]
    piece = init_basis.shape[2]
    per = piece // tile
    height = cols * piece
    length = rows * piece
    vmem = pltpu.VMEM
    tiles = pl.BlockSpec((cols, cap, tile, tile), lambda f: (f, 0, 0, 0))
    real, imag, rdeg, cdeg = pl.pallas_call(
        functools.partial(prep_kernel, cols, cap, per, tile),
        grid=(rows,),
        in_specs=[pl.BlockSpec(memory_space=pltpu.SMEM)] * 2 + [tiles, tiles],
        out_specs=[
            pl.BlockSpec((height, piece), lambda f: (0, f)),
            pl.BlockSpec((height, piece), lambda f: (0, f)),
            pl.BlockSpec((cols, 8, piece), lambda f: (0, 0, 0)),
            pl.BlockSpec((1, 8, piece), lambda f: (f, 0, 0)),
        ],
        out_shape=[
            jax.ShapeDtypeStruct((height, length), jnp.bfloat16),
            jax.ShapeDtypeStruct((height, length), jnp.bfloat16),
            jax.ShapeDtypeStruct((cols, 8, piece), jnp.float32),
            jax.ShapeDtypeStruct((rows, 8, piece), jnp.float32),
        ],
        scratch_shapes=[vmem((piece, piece), jnp.bfloat16)],
        name="prep",
    )(
        tile_list.reshape(devices * cap * 2),
        tile_count.reshape(devices),
        tile_weight.reshape(devices, cap, tile, tile),
        tile_angle.reshape(devices, cap, tile, tile),
    )
    side = 2 * width
    small = (width // 2, 4 * width)
    f32, bf16 = jnp.float32, jnp.bfloat16
    dma = pltpu.SemaphoreType.DMA
    anywhere = pl.BlockSpec(memory_space=pl.ANY)
    local = pl.BlockSpec(memory_space=pltpu.VMEM)
    out = pl.pallas_call(
        functools.partial(main_kernel, rows, cols, float(piece * devices), width),
        in_specs=[anywhere, anywhere, local, local, local],
        out_specs=local,
        out_shape=jax.ShapeDtypeStruct((side, piece), f32),
        scratch_shapes=[
            vmem((height, length), bf16), vmem((height, length), bf16),
            vmem((cols, 8, piece), f32), vmem((rows, 8, piece), f32),
            vmem((side, piece), bf16), vmem((rows, side, piece), bf16), vmem((cols, side, piece), bf16),
            vmem((cols, side, piece), PART_DTYPE), vmem((cols, side, piece), PART_DTYPE),
            vmem((rows, side, piece), PART_DTYPE), vmem((rows, side, piece), PART_DTYPE),
            vmem(small, f32), vmem((rows,) + small, f32), vmem(small, f32), vmem((cols,) + small, f32),
            vmem((side, piece), f32), vmem((8, piece), f32),
            dma((2,)),
            dma((rows,)), dma((rows,)), dma((cols,)), dma((cols,)),
            dma((rows,)), dma((rows,)), dma((cols,)), dma((cols,)),
            dma((cols,)), dma((cols,)), dma((rows,)), dma((rows,)),
            dma((rows,)), dma((rows,)), dma((cols,)), dma((cols,)),
        ],
        compiler_params=pltpu.CompilerParams(
            collective_id=0, has_side_effects=True, vmem_limit_bytes=60 * 1024 * 1024
        ),
        name="main",
    )(real, imag, rdeg, cdeg, init_basis.reshape(side, piece))
    return out.reshape(2, width, piece)


def solution(mesh):
    placed = (
        P(("row", "col"), None, None, None, None),
        P(("row", "col"), None, None, None, None),
        P(("row", "col"), None, None, None),
        P(("row", "col"), None),
        P(None, None, ("row", "col")),
    )
    return jax.shard_map(
        shards, mesh=mesh, in_specs=placed, out_specs=P(None, None, ("row", "col")), check_vma=False
    )
```

```python
import functools
import jax
import jax.numpy as jnp
from jax import lax
from jax.experimental import pallas as pl
from jax.experimental.pallas import tpu as pltpu
from jax.sharding import PartitionSpec as P

ITERS = 3
PART_DTYPE = jnp.bfloat16
MESH = pl.DeviceIdType.MESH
HIGH = lax.Precision.HIGHEST
NT = (((1,), (1,)), ((), ()))
NN = (((1,), (0,)), ((), ()))

SIN_TERMS = (-1.0 / 39916800, 1.0 / 362880, -1.0 / 5040, 1.0 / 120, -1.0 / 6, 1.0)
COS_TERMS = (1.0 / 479001600, -1.0 / 3628800, 1.0 / 40320, -1.0 / 720, 1.0 / 24, -0.5, 1.0)


def horner(terms, x):
    total = jnp.full_like(x, terms[0])
    for term in terms[1:]:
        total = total * x + term
    return total


def dot(left, right, dims, precision=None):
    return lax.dot_general(left, right, dims, precision=precision, preferred_element_type=jnp.float32)


def prep_kernel(cols, cap, per, tile, list_ref, count_ref, weight_ref, angle_ref, real_ref, imag_ref, rdeg_ref, cdeg_ref, held):
    f = pl.program_id(0)
    piece = per * tile

    @pl.when(f == 0)
    def _():
        rdeg_ref[...] = jnp.zeros_like(rdeg_ref)

    real_ref[...] = jnp.zeros_like(real_ref)
    imag_ref[...] = jnp.zeros_like(imag_ref)
    held[...] = jnp.zeros_like(held)

    def step(e, carry):
        d = f * cols + e
        for k in range(cap):

            @pl.when(k < count_ref[d])
            def _():
                at = (d * cap + k) * 2
                row_off = lax.rem(list_ref[at], per)
                col_off = lax.rem(list_ref[at + 1], per)
                weight = weight_ref[e, k]
                w = weight.astype(jnp.float32)
                half = angle_ref[e, k].astype(jnp.float32) * 0.5
                square = half * half
                sin_half = half * horner(SIN_TERMS, square)
                cos_half = horner(COS_TERMS, square)
                cos_full = 1.0 - 2.0 * (sin_half * sin_half)
                sin_full = 2.0 * (sin_half * cos_half)
                rows = pl.ds(pl.multiple_of(e * piece + row_off * tile, tile), tile)
                lanes = pl.ds(pl.multiple_of(col_off * tile, tile), tile)
                real_ref[rows, lanes] = (w * cos_full).astype(jnp.bfloat16)
                imag_ref[rows, lanes] = (w * sin_full).astype(jnp.bfloat16)
                held[rows, lanes] = weight

        return carry

    lax.fori_loop(0, cols, step, 0)
    across = jnp.ones((8, piece), jnp.bfloat16)
    down = jnp.ones((8, cols * piece), jnp.bfloat16)
    cdeg_ref[0] = dot(down, held[...], NN)
    for e in range(cols):
        rdeg_ref[e] += dot(across, held[e * piece:(e + 1) * piece], NT)


def main_kernel(
    rows, cols, images_all, width, real_any, imag_any, rdeg_ref, cdeg_ref, init_ref, out_ref,
    real, imag, rdeg_recv, cdeg_recv, xsend, xrow, xcol, fsend, frecv, msend, mrecv,
    grow_send, grow, gcol_send, gcol, basis, scales,
    load_sem, drs, drr, dcs, dcr, xrs, xrr, xcs, xcr, fs, fr, ms, mr_, grs, grr, gcs, gcr,
):
    a = lax.axis_index("row")
    b = lax.axis_index("col")
    piece = init_ref.shape[1]

    def row_peer(k):
        return lax.rem(a + k, rows)

    def col_peer(k):
        return lax.rem(b + k, cols)

    def row_copy(src, dst, ssem, rsem, k):
        return pltpu.make_async_remote_copy(
            src_ref=src, dst_ref=dst.at[a], send_sem=ssem.at[k], recv_sem=rsem.at[k],
            device_id=(row_peer(k), b), device_id_type=MESH)

    def col_copy(src, dst, ssem, rsem, k):
        return pltpu.make_async_remote_copy(
            src_ref=src, dst_ref=dst.at[b], send_sem=ssem.at[k], recv_sem=rsem.at[k],
            device_id=(a, col_peer(k)), device_id_type=MESH)

    loads = [pltpu.make_async_copy(real_any, real, load_sem.at[0]),
             pltpu.make_async_copy(imag_any, imag, load_sem.at[1])]
    for load in loads:
        load.start()

    barrier = pltpu.get_barrier_semaphore()
    for k in range(1, rows):
        pl.semaphore_signal(barrier, inc=1, device_id=(row_peer(k), b), device_id_type=MESH)
    for k in range(1, cols):
        pl.semaphore_signal(barrier, inc=1, device_id=(a, col_peer(k)), device_id_type=MESH)
    pl.semaphore_wait(barrier, rows + cols - 2)

    copies = [col_copy(rdeg_ref.at[col_peer(k)], rdeg_recv, dcs, dcr, k) for k in range(1, cols)]
    copies += [row_copy(cdeg_ref.at[row_peer(k)], cdeg_recv, drs, drr, k) for k in range(1, rows)]
    for copy in copies:
        copy.start()
    rdeg_recv[b] = rdeg_ref[b]
    cdeg_recv[a] = cdeg_ref[a]
    basis[...] = init_ref[...]
    for copy in copies:
        copy.wait()
    degree = rdeg_recv[0]
    for e in range(1, cols):
        degree = degree + rdeg_recv[e]
    for f in range(rows):
        degree = degree + cdeg_recv[f]
    scales[...] = 1.0 / jnp.sqrt(0.5 * degree)
    for load in loads:
        load.wait()

    def turned(x):
        return jnp.concatenate([-x[width:], x[:width]], 0)

    row_id = lax.broadcasted_iota(jnp.int32, (width, 4 * width), 0)
    lane_id = lax.broadcasted_iota(jnp.int32, (width, 4 * width), 1)

    def iteration(t, carry):
        scale = scales[0:1]
        xs = (basis[...] * scale).astype(jnp.bfloat16)
        xsend[...] = xs
        row_x = [row_copy(xsend, xrow, xrs, xrr, k) for k in range(1, rows)]
        col_x = [col_copy(xsend, xcol, xcs, xcr, k) for k in range(1, cols)]
        for copy in row_x + col_x:
            copy.start()
        xrow[a] = xs
        xcol[b] = xs
        for copy in row_x:
            copy.wait_recv()

        def forward(e):
            total = None
            at = pl.ds(pl.multiple_of(e * piece, piece), piece)
            for f in range(rows):
                x = xrow[f]
                lanes = slice(f * piece, (f + 1) * piece)
                term = dot(x, real[at, lanes], NT) + dot(turned(x), imag[at, lanes], NT)
                total = term if total is None else total + term
            return total.astype(fsend.dtype)

        def forward_step(k, carry):
            fsend[k] = forward(col_peer(k))
            col_copy(fsend.at[k], frecv, fs, fr, k).start()
            return carry

        lax.fori_loop(1, cols, forward_step, 0)
        frecv[b] = forward(b)
        for copy in col_x:
            copy.wait_recv()

        def mirror(f):
            total = None
            lanes = pl.ds(pl.multiple_of(f * piece, piece), piece)
            for e in range(cols):
                x = xcol[e]
                at = slice(e * piece, (e + 1) * piece)
                term = dot(x, real[at, lanes], NN) - dot(turned(x), imag[at, lanes], NN)
                total = term if total is None else total + term
            return total.astype(msend.dtype)

        def mirror_step(k, carry):
            msend[k] = mirror(row_peer(k))
            row_copy(msend.at[k], mrecv, ms, mr_, k).start()
            return carry

        lax.fori_loop(1, rows, mirror_step, 0)
        mrecv[a] = mirror(a)
        for copy in row_x + col_x:
            copy.wait_send()
        for k in range(1, cols):
            col_copy(fsend.at[k], frecv, fs, fr, k).wait()
        for k in range(1, rows):
            row_copy(msend.at[k], mrecv, ms, mr_, k).wait()
        total = frecv[0].astype(jnp.float32)
        for e in range(1, cols):
            total = total + frecv[e].astype(jnp.float32)
        for f in range(rows):
            total = total + mrecv[f].astype(jnp.float32)
        image = total * (0.5 * scale)

        first, second = image[:width], image[width:]
        both = jnp.concatenate([first, second], 1)
        other = jnp.concatenate([second, -first], 1)
        right = jnp.concatenate([both, other, jnp.zeros((2 * width, 2 * piece), jnp.float32)], 0)
        gram = dot(both, right, NT, HIGH)
        upper = width // 2
        packed = gram[:upper] + pltpu.roll(gram[upper:], 2 * width, 1)
        grow_send[...] = packed
        gram_row = [row_copy(grow_send, grow, grs, grr, k) for k in range(1, rows)]
        for copy in gram_row:
            copy.start()
        grow[a] = packed
        for copy in gram_row:
            copy.wait()
        packed = grow[0]
        for f in range(1, rows):
            packed = packed + grow[f]
        gcol_send[...] = packed
        gram_col = [col_copy(gcol_send, gcol, gcs, gcr, k) for k in range(1, cols)]
        for copy in gram_col:
            copy.start()
        gcol[b] = packed
        for copy in gram_col:
            copy.wait()
        packed = gcol[0]
        for e in range(1, cols):
            packed = packed + gcol[e]
        packed = packed / images_all
        gram = jnp.concatenate([packed, pltpu.roll(packed, 2 * width, 1)], 0)
        inside = lane_id < width
        on_diag = lane_id == row_id
        trace = jnp.sum(jnp.where(on_diag, gram, 0.0), axis=(0, 1), keepdims=True)
        ridge = 0.01 * trace / width + 1e-06
        ar = jnp.where(inside, gram, jnp.where(lane_id == row_id + width, 1.0, 0.0))
        ar = ar + jnp.where(on_diag, ridge, 0.0)
        ai = jnp.where(inside, pltpu.roll(gram, 3 * width, 1), 0.0)
        for c in range(width):
            below = row_id[:, 0:1] > c
            inverse = 1.0 / ar[c:c + 1, c:c + 1]
            fac_r = jnp.where(below, ar[:, c:c + 1], 0.0)
            fac_i = jnp.where(below, ai[:, c:c + 1], 0.0)
            top_r = ar[c:c + 1] * inverse
            top_i = ai[c:c + 1] * inverse
            ar = ar - (fac_r * top_r - fac_i * top_i)
            ai = ai - (fac_r * top_i + fac_i * top_r)
        pivots = jnp.sum(jnp.where(on_diag, ar, 0.0), axis=1, keepdims=True)
        roots = 1.0 / jnp.sqrt(pivots)
        ar = ar * roots
        ai = ai * roots
        top = jnp.where(inside, pltpu.roll(ar, 3 * width, 1), ai)
        bottom = jnp.where(inside, -pltpu.roll(ai, 3 * width, 1), ar)
        left = jnp.concatenate([top, bottom], 0)[:, :2 * width]
        basis[...] = dot(left, image, NN, HIGH)
        return carry

    lax.fori_loop(0, ITERS, iteration, 0)
    out_ref[...] = basis[...]


def shards(tile_weight, tile_angle, tile_list, tile_count, init_basis):
    rows = lax.axis_size("row")
    cols = lax.axis_size("col")
    devices = rows * cols
    tile = tile_weight.shape[-1]
    cap = tile_weight.shape[2]
    width = init_basis.shape[1]
    piece = init_basis.shape[2]
    per = piece // tile
    height = cols * piece
    length = rows * piece
    vmem = pltpu.VMEM
    tiles = pl.BlockSpec((cols, cap, tile, tile), lambda f: (f, 0, 0, 0))
    real, imag, rdeg, cdeg = pl.pallas_call(
        functools.partial(prep_kernel, cols, cap, per, tile),
        grid=(rows,),
        in_specs=[pl.BlockSpec(memory_space=pltpu.SMEM)] * 2 + [tiles, tiles],
        out_specs=[
            pl.BlockSpec((height, piece), lambda f: (0, f)),
            pl.BlockSpec((height, piece), lambda f: (0, f)),
            pl.BlockSpec((cols, 8, piece), lambda f: (0, 0, 0)),
            pl.BlockSpec((1, 8, piece), lambda f: (f, 0, 0)),
        ],
        out_shape=[
            jax.ShapeDtypeStruct((height, length), jnp.bfloat16),
            jax.ShapeDtypeStruct((height, length), jnp.bfloat16),
            jax.ShapeDtypeStruct((cols, 8, piece), jnp.float32),
            jax.ShapeDtypeStruct((rows, 8, piece), jnp.float32),
        ],
        scratch_shapes=[vmem((height, piece), jnp.bfloat16)],
        name="prep",
    )(
        tile_list.reshape(devices * cap * 2),
        tile_count.reshape(devices),
        tile_weight.reshape(devices, cap, tile, tile),
        tile_angle.reshape(devices, cap, tile, tile),
    )
    side = 2 * width
    small = (width // 2, 4 * width)
    f32, bf16 = jnp.float32, jnp.bfloat16
    dma = pltpu.SemaphoreType.DMA
    anywhere = pl.BlockSpec(memory_space=pl.ANY)
    local = pl.BlockSpec(memory_space=pltpu.VMEM)
    out = pl.pallas_call(
        functools.partial(main_kernel, rows, cols, float(piece * devices), width),
        in_specs=[anywhere, anywhere, local, local, local],
        out_specs=local,
        out_shape=jax.ShapeDtypeStruct((side, piece), f32),
        scratch_shapes=[
            vmem((height, length), bf16), vmem((height, length), bf16),
            vmem((cols, 8, piece), f32), vmem((rows, 8, piece), f32),
            vmem((side, piece), bf16), vmem((rows, side, piece), bf16), vmem((cols, side, piece), bf16),
            vmem((cols, side, piece), PART_DTYPE), vmem((cols, side, piece), PART_DTYPE),
            vmem((rows, side, piece), PART_DTYPE), vmem((rows, side, piece), PART_DTYPE),
            vmem(small, f32), vmem((rows,) + small, f32), vmem(small, f32), vmem((cols,) + small, f32),
            vmem((side, piece), f32), vmem((8, piece), f32),
            dma((2,)),
            dma((rows,)), dma((rows,)), dma((cols,)), dma((cols,)),
            dma((rows,)), dma((rows,)), dma((cols,)), dma((cols,)),
            dma((cols,)), dma((cols,)), dma((rows,)), dma((rows,)),
            dma((rows,)), dma((rows,)), dma((cols,)), dma((cols,)),
        ],
        compiler_params=pltpu.CompilerParams(
            collective_id=0, has_side_effects=True, vmem_limit_bytes=60 * 1024 * 1024
        ),
        name="main",
    )(real, imag, rdeg, cdeg, init_basis.reshape(side, piece))
    return out.reshape(2, width, piece)


def solution(mesh):
    placed = (
        P(("row", "col"), None, None, None, None),
        P(("row", "col"), None, None, None, None),
        P(("row", "col"), None, None, None),
        P(("row", "col"), None),
        P(None, None, ("row", "col")),
    )
    return jax.shard_map(
        shards, mesh=mesh, in_specs=placed, out_specs=P(None, None, ("row", "col")), check_vma=False
    )
```
